32 devices in a mesh: groups: 2 (over x), seq: 16 (over z, y, core).
Axes of the slice: x: 2, y: 2, z: 4, core: 2. Of those that a mesh axis runs over, the one named last changes fastest.
Arguments:
- video: bfloat16 [32, 32, 1408], P(('groups', 'seq')), parts along dimension 0, may hold values from -6 to 6
- spatial_qkv: bfloat16 [1408, 2112], P('seq'), may hold values from -1 to 1
- spatial_out: bfloat16 [704, 1408], P(None, 'seq'), may hold values from -0.21875 to 0.21875
- temporal_qkv: bfloat16 [1408, 2112], P('seq'), may hold values from -1 to 1
- temporal_out: bfloat16 [704, 1408], P(None, 'seq'), may hold values from -0.21875 to 0.21875
Outputs:
- result: bfloat16 [32, 32, 1408], P(('groups', 'seq')), parts along dimension 0
The draws below stay inside these ranges and needn't reach their ends.
There are 2 independent parts, one for each index of `groups`. The reference program is written for one: setup_inputs(seed, part) draws one part's arguments, and reference() takes and returns one part's arrays. A program takes and returns all parts, laid end to end along the dimension named above; an argument that names none is the same for every part. Nothing has to cross between parts.
All inputs are finite; a program needn't handle non-finite values.
Results may differ from the reference program's by a relative error of at most 0.0065.
Values may be sent and summed in bfloat16 or wider, within the bound.
No kernel may reach another device: no remote copies, remote signals or barrier semaphores. Data moves between devices by JAX's collectives and lax.ppermute only.
A program may use at most 128 MiB of HBM per device.

```python
import jax
import jax.numpy as jnp
from jax import lax

D = 1408
HEADS = 8
HEAD_DIM = 88
FRAMES = 16
PATCHES = 32
HD = 704


def projection_draw(key):
    head_total = HEADS * HEAD_DIM
    first_key = jax.random.fold_in(key, 0)
    drawn = jax.random.normal(first_key, (D, 3 * head_total), jnp.float32) * D ** (-0.5)
    return jnp.clip(drawn, -1.0, 1.0)


def draw_spatial_qkv(key, part):
    return projection_draw(jax.random.fold_in(key, 11)).astype(jnp.bfloat16)


def draw_temporal_qkv(key, part):
    return projection_draw(jax.random.fold_in(key, 23)).astype(jnp.bfloat16)


def levels(rng, dims, cuts, low, largest):
    def one(position, parts):
        draws = jax.random.uniform(jax.random.fold_in(jax.random.fold_in(rng, 6), position), (parts,), jnp.float32, low / len(cuts), largest / len(cuts))
        return jnp.repeat(jnp.exp(draws), dims[position] // parts).reshape((-1,) + (1,) * (len(dims) - position - 1))

    level = one(*cuts[0])
    for cut in cuts[1:]:
        level = level * one(*cut)
    return level


def gaussian(rng, shape, deviation, most, cuts=(), held_as=jnp.bfloat16):
    gain = levels(rng, shape, cuts, -0.22, 0.18) if cuts else 1.0
    values = jax.random.normal(rng, shape, jnp.float32) * deviation * gain
    return jnp.minimum(jnp.maximum(values, -most), most).astype(held_as)


def setup_inputs(seed: int = 0, part: int = 0) -> dict:
    arg_keys = jax.random.split(jax.random.key(seed), 6)
    part_keys = jax.random.split(jax.random.fold_in(arg_keys[5], part), 6)
    return {
        "video": gaussian(part_keys[0], (FRAMES, PATCHES, D), 1.0, 6.0, ((0, 16),)),
        "spatial_qkv": draw_spatial_qkv(jax.random.fold_in(arg_keys[5], 71), part),
        "spatial_out": gaussian(arg_keys[2], (HD, D), HD ** -0.5, 0.21875, ((1, 16),)),
        "temporal_qkv": draw_temporal_qkv(jax.random.fold_in(arg_keys[5], 71), part),
        "temporal_out": gaussian(arg_keys[4], (HD, D), HD ** -0.5, 0.21875, ((1, 16),)),
    }


def normalize(tokens):
    values = tokens.astype(jnp.float32)
    center = values - lax.optimization_barrier(jnp.mean(values, axis=-1, keepdims=True))
    variance = lax.optimization_barrier(jnp.mean(center * center, axis=-1, keepdims=True))
    return (center * lax.rsqrt(variance + 1e-06)).astype(jnp.bfloat16)

def attend(queries, keys_in, values_in):
    scores = jnp.einsum('qhe,khe->hqk', queries.astype(jnp.float32), keys_in.astype(jnp.float32)) * HEAD_DIM ** (-0.5)
    weights = jax.nn.softmax(scores, axis=-1).astype(jnp.bfloat16)
    return jnp.einsum('hqk,khe->qhe', weights.astype(jnp.float32), values_in.astype(jnp.float32)).astype(jnp.bfloat16)

def one_group(grouped):
    return attend(grouped[:, 0], grouped[:, 1], grouped[:, 2])

def reference(video, spatial_qkv, spatial_out, temporal_qkv, temporal_out):
    head_total = HEADS * HEAD_DIM
    flat = video.reshape(-1, D)
    normed = normalize(flat)
    packed = jnp.dot(normed, spatial_qkv, preferred_element_type=jnp.float32).astype(jnp.bfloat16)
    packed = packed.reshape(FRAMES, PATCHES, 3, HEADS, HEAD_DIM)
    spatial = lax.map(one_group, packed).reshape(-1, head_total)
    mixed = (flat.astype(jnp.float32) + jnp.dot(spatial, spatial_out, preferred_element_type=jnp.float32)).astype(jnp.bfloat16)
    normed_two = normalize(mixed)
    packed_two = jnp.dot(normed_two, temporal_qkv, preferred_element_type=jnp.float32).astype(jnp.bfloat16)
    packed_two = packed_two.reshape(FRAMES, PATCHES, 3, HEADS, HEAD_DIM).transpose(1, 0, 2, 3, 4)
    temporal = lax.map(one_group, packed_two).transpose(1, 0, 2, 3).reshape(-1, head_total)
    result = mixed.astype(jnp.float32) + jnp.dot(temporal, temporal_out, preferred_element_type=jnp.float32)
    return result.astype(jnp.bfloat16).reshape(FRAMES, PATCHES, D)
```

```python
import jax
import jax.numpy as jnp
from jax import lax
from jax.experimental import pallas as pl
from jax.experimental.pallas import tpu as pltpu
from jax.sharding import PartitionSpec as P

HEADS = 8
HEAD_DIM = 88


def normalize(tokens):
    values = tokens.astype(jnp.float32)
    center = values - jnp.mean(values, axis=-1, keepdims=True)
    variance = jnp.mean(center * center, axis=-1, keepdims=True)
    return (center * lax.rsqrt(variance + 1e-06)).astype(jnp.bfloat16)


def attend(queries, keys_in, values_in):
    scores = jnp.einsum(
        "bqhe,bkhe->bhqk", queries, keys_in, preferred_element_type=jnp.float32
    ) * HEAD_DIM ** (-0.5)
    weights = jax.nn.softmax(scores, axis=-1).astype(jnp.bfloat16)
    return jnp.einsum(
        "bhqk,bkhe->bqhe", weights, values_in, preferred_element_type=jnp.float32
    ).astype(jnp.bfloat16)


def gathered_weights_body(video, spatial_qkv, spatial_out, temporal_qkv, temporal_out):
    frames, patches, model_width = video.shape
    head_total = HEADS * HEAD_DIM
    flat = video.reshape(-1, model_width)
    normed = normalize(flat)
    gathered = (
        lax.all_gather(spatial_qkv, "seq", axis=0, tiled=True),
        lax.all_gather(spatial_out, "seq", axis=1, tiled=True),
        lax.all_gather(temporal_qkv, "seq", axis=0, tiled=True),
        lax.all_gather(temporal_out, "seq", axis=1, tiled=True),
    )
    packed = (
        jnp.dot(normed, gathered[0], preferred_element_type=jnp.float32)
        .astype(jnp.bfloat16)
        .reshape(frames, patches, 3, HEADS, HEAD_DIM)
    )
    spatial = attend(packed[:, :, 0], packed[:, :, 1], packed[:, :, 2]).reshape(-1, head_total)
    mixed = (
        flat.astype(jnp.float32) + jnp.dot(spatial, gathered[1], preferred_element_type=jnp.float32)
    ).astype(jnp.bfloat16)
    mixed = mixed.reshape(frames, patches, model_width)
    moved = lax.all_to_all(mixed, "seq", split_axis=1, concat_axis=0, tiled=True)
    all_frames, local_patches = (moved.shape[0], moved.shape[1])
    normed_two = normalize(moved.reshape(-1, model_width))
    packed_two = jnp.dot(normed_two, gathered[2], preferred_element_type=jnp.float32).astype(
        jnp.bfloat16
    )
    packed_two = packed_two.reshape(all_frames, local_patches, 3, HEADS, HEAD_DIM).transpose(
        1, 0, 2, 3, 4
    )
    temporal = attend(packed_two[:, :, 0], packed_two[:, :, 1], packed_two[:, :, 2])
    temporal = temporal.transpose(1, 0, 2, 3).reshape(all_frames, local_patches, head_total)
    update = jnp.dot(
        temporal.reshape(-1, head_total), gathered[3], preferred_element_type=jnp.float32
    ).reshape(all_frames, local_patches, model_width)
    finished = (moved.astype(jnp.float32) + update).astype(jnp.bfloat16)
    return lax.all_to_all(finished, "seq", split_axis=0, concat_axis=1, tiled=True)


COLUMNS = [[4 * z + 2 * y + k for z in range(4) for k in range(2)] for y in range(2)]
ACROSS_Y = [(i, i ^ 2) for i in range(16)]


def pack(w):
    w = w.reshape(11, 8, 3, HEADS, HEAD_DIM)
    return w.transpose(3, 1, 0, 2, 4).reshape(HEADS, 8, 11 * 3 * HEAD_DIM)


def unpack(y, mine_ref, theirs_ref, wide_ref):
    for half, ref in ((y, mine_ref), (1 - y, theirs_ref)):
        for j in range(8):
            slab = ref[j].astype(jnp.float32)
            first = pl.multiple_of(88 * (4 * (j // 2) + 2 * half + j % 2), 8)
            for g in range(11):
                wide_ref[pl.ds(first + 8 * g, 8), :] = slab[:, 264 * g : 264 * (g + 1)]
    return wide_ref[...].astype(jnp.bfloat16)


def masked_attention(packed, same):
    q, k, v = packed[:, :88], packed[:, 88:176], packed[:, 176:]
    scores = lax.dot_general(q, k, (((1,), (1,)), ((), ())), preferred_element_type=jnp.float32) * HEAD_DIM ** (-0.5)
    scores = jnp.where(same, scores, -jnp.inf)
    top = jnp.max(scores, axis=-1, keepdims=True)
    e = jnp.exp(scores - top)
    weights = (e / jnp.sum(e, axis=-1, keepdims=True)).astype(jnp.bfloat16)
    return jnp.dot(weights, v, preferred_element_type=jnp.float32).astype(jnp.bfloat16)


def spatial_kernel(y_ref, tokens_ref, mine_ref, theirs_ref, out_ref, wide_ref):
    w = unpack(y_ref[0], mine_ref, theirs_ref, wide_ref)
    packed = jnp.dot(normalize(tokens_ref[...]), w, preferred_element_type=jnp.float32).astype(jnp.bfloat16)
    n = packed.shape[0]
    row = lax.broadcasted_iota(jnp.int32, (n, n), 0) // 32
    col = lax.broadcasted_iota(jnp.int32, (n, n), 1) // 32
    out_ref[...] = masked_attention(packed, row == col)


def middle_kernel(y_ref, tokens_ref, spatial_ref, out_one_ref, mine_ref, theirs_ref, mixed_ref, two_ref, wide_ref):
    w = unpack(y_ref[0], mine_ref, theirs_ref, wide_ref)
    heads = jnp.concatenate([spatial_ref[h] for h in range(8)], axis=1)
    update = lax.dot_general(heads, out_one_ref[...], (((1,), (1,)), ((), ())), preferred_element_type=jnp.float32)
    mixed = (tokens_ref[...].astype(jnp.float32) + update).astype(jnp.bfloat16)
    mixed_ref[...] = mixed
    two_ref[...] = jnp.dot(normalize(mixed), w, preferred_element_type=jnp.float32).astype(jnp.bfloat16)


def temporal_kernel(packed_ref, out_ref):
    n = packed_ref.shape[0]
    row = lax.broadcasted_iota(jnp.int32, (n, n), 0) % 16
    col = lax.broadcasted_iota(jnp.int32, (n, n), 1) % 16
    out_ref[...] = masked_attention(packed_ref[...], row == col)


VM = pl.BlockSpec(memory_space=pltpu.VMEM)
SM = pl.BlockSpec(memory_space=pltpu.SMEM)


def kernel_call(body, shapes, n_in, scratch=(), scalar=False):
    return pl.pallas_call(
        body,
        out_shape=shapes,
        in_specs=([SM] if scalar else []) + [VM] * n_in,
        out_specs=jax.tree.map(lambda _: VM, shapes),
        scratch_shapes=scratch,
        compiler_params=pltpu.CompilerParams(vmem_limit_bytes=40 * 1024 * 1024),
    )


def head_body(video, spatial_qkv, spatial_out, temporal_qkv, temporal_out):
    _, patches, D = video.shape
    bf = jnp.bfloat16
    y = (lax.axis_index("seq") // 2) % 2
    ys = y.reshape(1)
    out_one = lax.all_gather(spatial_out.T, "seq", axis=0, tiled=True)
    one = lax.all_to_all(pack(spatial_qkv), "seq", 0, 0, tiled=True, axis_index_groups=COLUMNS)
    tokens = lax.all_gather(video.reshape(patches, D), "seq", axis=0, tiled=True, axis_index_groups=COLUMNS)
    one, tokens, two_p = lax.optimization_barrier((one, tokens, pack(temporal_qkv)))
    one_o = lax.ppermute(one, "seq", ACROSS_Y)
    two_w = lax.all_to_all(two_p, "seq", 0, 0, tiled=True, axis_index_groups=COLUMNS)
    wide = [pltpu.VMEM((D, 264), jnp.float32)]
    spatial = kernel_call(spatial_kernel, jax.ShapeDtypeStruct((256, 88), bf), 3, wide, True)(ys, tokens, one, one_o)
    spatial, two_w, t_out = lax.optimization_barrier((spatial, two_w, temporal_out.T))
    out_two = lax.all_gather(t_out, "seq", axis=0, tiled=True)
    two_o = lax.ppermute(two_w, "seq", ACROSS_Y)
    spatial = lax.all_gather(spatial, "seq", axis=0, tiled=False, axis_index_groups=COLUMNS)
    mixed, two = kernel_call(
        middle_kernel, (jax.ShapeDtypeStruct((256, D), bf), jax.ShapeDtypeStruct((256, 264), bf)), 5, wide, True
    )(ys, tokens, spatial, out_one, two_w, two_o)
    two = two.reshape(8, 2, patches // 2, 264)
    keep = jnp.where(y == 0, two[:, 0], two[:, 1])
    send = jnp.where(y == 0, two[:, 1], two[:, 0])
    other = lax.ppermute(send, "seq", ACROSS_Y)
    both = jnp.where(y == 0, jnp.stack([keep, other], 1), jnp.stack([other, keep], 1))
    both = both.reshape(4, 2, 2, patches // 2, 264).transpose(0, 2, 1, 3, 4).reshape(256, 264)
    temporal = kernel_call(temporal_kernel, jax.ShapeDtypeStruct((256, 88), bf), 1)(both).reshape(16, patches // 2, 88)
    temporal = lax.all_to_all(temporal, "seq", 0, 0, tiled=True)
    temporal = temporal.reshape(4, 2, 2, patches // 2, 88).transpose(1, 3, 0, 2, 4).reshape(patches, 704)
    me = 2 * (lax.axis_index("seq") // 4) + lax.axis_index("seq") % 2
    own = lax.dynamic_slice_in_dim(mixed, me * patches, patches, axis=0)
    result = own.astype(jnp.float32) + lax.dot_general(temporal, out_two, (((1,), (1,)), ((), ())), preferred_element_type=jnp.float32)
    return result.astype(jnp.bfloat16).reshape(1, patches, D)


def solution(mesh):
    in_specs = (
        P(("groups", "seq"), None, None),
        P("seq", None),
        P(None, "seq"),
        P("seq", None),
        P(None, "seq"),
    )
    out_specs = P(("groups", "seq"), None, None)
    body = head_body if mesh.shape["seq"] == 16 else gathered_weights_body
    return jax.shard_map(body, mesh=mesh, in_specs=in_specs, out_specs=out_specs, check_vma=False)
```

```python
import jax
import jax.numpy as jnp
from jax import lax
from jax.experimental import pallas as pl
from jax.experimental.pallas import tpu as pltpu
from jax.sharding import PartitionSpec as P

HEADS = 8
HEAD_DIM = 88


def normalize(tokens):
    values = tokens.astype(jnp.float32)
    center = values - jnp.mean(values, axis=-1, keepdims=True)
    variance = jnp.mean(center * center, axis=-1, keepdims=True)
    return (center * lax.rsqrt(variance + 1e-06)).astype(jnp.bfloat16)


def attend(queries, keys_in, values_in):
    scores = jnp.einsum(
        "bqhe,bkhe->bhqk", queries, keys_in, preferred_element_type=jnp.float32
    ) * HEAD_DIM ** (-0.5)
    weights = jax.nn.softmax(scores, axis=-1).astype(jnp.bfloat16)
    return jnp.einsum(
        "bhqk,bkhe->bqhe", weights, values_in, preferred_element_type=jnp.float32
    ).astype(jnp.bfloat16)


def gathered_weights_body(video, spatial_qkv, spatial_out, temporal_qkv, temporal_out):
    frames, patches, model_width = video.shape
    head_total = HEADS * HEAD_DIM
    flat = video.reshape(-1, model_width)
    normed = normalize(flat)
    gathered = (
        lax.all_gather(spatial_qkv, "seq", axis=0, tiled=True),
        lax.all_gather(spatial_out, "seq", axis=1, tiled=True),
        lax.all_gather(temporal_qkv, "seq", axis=0, tiled=True),
        lax.all_gather(temporal_out, "seq", axis=1, tiled=True),
    )
    packed = (
        jnp.dot(normed, gathered[0], preferred_element_type=jnp.float32)
        .astype(jnp.bfloat16)
        .reshape(frames, patches, 3, HEADS, HEAD_DIM)
    )
    spatial = attend(packed[:, :, 0], packed[:, :, 1], packed[:, :, 2]).reshape(-1, head_total)
    mixed = (
        flat.astype(jnp.float32) + jnp.dot(spatial, gathered[1], preferred_element_type=jnp.float32)
    ).astype(jnp.bfloat16)
    mixed = mixed.reshape(frames, patches, model_width)
    moved = lax.all_to_all(mixed, "seq", split_axis=1, concat_axis=0, tiled=True)
    all_frames, local_patches = (moved.shape[0], moved.shape[1])
    normed_two = normalize(moved.reshape(-1, model_width))
    packed_two = jnp.dot(normed_two, gathered[2], preferred_element_type=jnp.float32).astype(
        jnp.bfloat16
    )
    packed_two = packed_two.reshape(all_frames, local_patches, 3, HEADS, HEAD_DIM).transpose(
        1, 0, 2, 3, 4
    )
    temporal = attend(packed_two[:, :, 0], packed_two[:, :, 1], packed_two[:, :, 2])
    temporal = temporal.transpose(1, 0, 2, 3).reshape(all_frames, local_patches, head_total)
    update = jnp.dot(
        temporal.reshape(-1, head_total), gathered[3], preferred_element_type=jnp.float32
    ).reshape(all_frames, local_patches, model_width)
    finished = (moved.astype(jnp.float32) + update).astype(jnp.bfloat16)
    return lax.all_to_all(finished, "seq", split_axis=0, concat_axis=1, tiled=True)


COLUMNS = [[4 * z + 2 * y + k for z in range(4) for k in range(2)] for y in range(2)]
ACROSS_Y = [(i, i ^ 2) for i in range(16)]


def pack(w):
    w = w.reshape(11, 8, 3, HEADS, HEAD_DIM)
    return w.transpose(3, 1, 0, 2, 4).reshape(HEADS, 8, 11 * 3 * HEAD_DIM)


def pack_kernel(w_ref, out_ref):
    for g in range(11):
        rows = w_ref[8 * g : 8 * (g + 1), :].astype(jnp.float32)
        for h in range(HEADS):
            for c in range(3):
                at = 264 * g + 88 * c
                piece = rows[:, 704 * c + 88 * h : 704 * c + 88 * (h + 1)]
                out_ref[h, :, at : at + 88] = piece.astype(jnp.bfloat16)


def pack_call(w):
    return kernel_call(pack_kernel, jax.ShapeDtypeStruct((HEADS, 8, 11 * 264), jnp.bfloat16), 1)(w)


def unpack(y, mine_ref, theirs_ref, wide_ref):
    for half, ref in ((y, mine_ref), (1 - y, theirs_ref)):
        for j in range(8):
            slab = ref[j].astype(jnp.float32)
            first = pl.multiple_of(88 * (4 * (j // 2) + 2 * half + j % 2), 8)
            for g in range(11):
                wide_ref[pl.ds(first + 8 * g, 8), :] = slab[:, 264 * g : 264 * (g + 1)]
    return wide_ref[...].astype(jnp.bfloat16)


def masked_attention(packed, same):
    q, k, v = packed[:, :88], packed[:, 88:176], packed[:, 176:]
    scores = lax.dot_general(q, k, (((1,), (1,)), ((), ())), preferred_element_type=jnp.float32) * HEAD_DIM ** (-0.5)
    scores = jnp.where(same, scores, -jnp.inf)
    top = jnp.max(scores, axis=-1, keepdims=True)
    e = jnp.exp(scores - top)
    weights = (e / jnp.sum(e, axis=-1, keepdims=True)).astype(jnp.bfloat16)
    return jnp.dot(weights, v, preferred_element_type=jnp.float32).astype(jnp.bfloat16)


def assemble(at_ref, same_ref, cross_ref, all_ref):
    z, k = at_ref[1], at_ref[2]
    for d in range(4):
        first = 2 * (z ^ d)
        all_ref[first + k] = same_ref[d]
        all_ref[first + 1 - k] = cross_ref[d]


def heads_of(all_ref):
    parts = []
    for r in range(4):
        parts.append(jnp.concatenate([all_ref[h][:, 88 * r : 88 * (r + 1)] for h in range(HEADS)], axis=1))
    return jnp.concatenate(parts, axis=0)


def fold(rows):
    return jnp.concatenate([rows[64 * r : 64 * (r + 1)] for r in range(4)], axis=1)


def tokens_kernel(at_ref, same_ref, cross_ref, normed_ref, picked_ref, all_ref):
    assemble(at_ref, same_ref, cross_ref, all_ref)
    y, z, k = at_ref[0], at_ref[1], at_ref[2]
    n = all_ref.shape[2]
    row = lax.broadcasted_iota(jnp.int32, (n, 176), 0)
    col = lax.broadcasted_iota(jnp.int32, (n, 176), 1)
    first = 88 * (4 * z + k)
    place = jnp.where(col < 88, first + col, first + 88 + col)
    chosen = (row == place).astype(jnp.float32).astype(jnp.bfloat16)
    tokens = jnp.concatenate([all_ref[j] for j in range(8)], axis=0)
    normed_ref[...] = normalize(tokens)
    picked_ref[...] = jnp.dot(tokens, chosen, preferred_element_type=jnp.float32).astype(jnp.bfloat16)


def spatial_kernel(at_ref, normed_ref, mine_ref, theirs_ref, out_ref, wide_ref):
    w = unpack(at_ref[0], mine_ref, theirs_ref, wide_ref)
    packed = jnp.dot(normed_ref[...], w, preferred_element_type=jnp.float32).astype(jnp.bfloat16)
    n = packed.shape[0]
    row = lax.broadcasted_iota(jnp.int32, (n, n), 0) // 32
    col = lax.broadcasted_iota(jnp.int32, (n, n), 1) // 32
    out_ref[...] = fold(masked_attention(packed, row == col))


def columns(y, own_ref, other_ref):
    own, other = own_ref[...], other_ref[...]
    return jnp.concatenate([jnp.where(y == 0, own, other), jnp.where(y == 0, other, own)], axis=1)


def mixed_kernel(at_ref, same_ref, cross_ref, picked_ref, own_ref, other_ref, keep_ref, send_ref, all_ref):
    y = at_ref[0]
    assemble(at_ref, same_ref, cross_ref, all_ref)
    update = jnp.dot(heads_of(all_ref), columns(y, own_ref, other_ref), preferred_element_type=jnp.float32)
    mixed = picked_ref[...].astype(jnp.float32) + update
    for j in range(8):
        low, high = mixed[32 * j : 32 * j + 16], mixed[32 * j + 16 : 32 * j + 32]
        keep_ref[16 * j : 16 * j + 16, :] = jnp.where(y == 0, low, high).astype(jnp.bfloat16)
        send_ref[16 * j : 16 * j + 16, :] = jnp.where(y == 0, high, low).astype(jnp.bfloat16)


def rows_kernel(at_ref, mine_ref, theirs_ref, out_ref, wide_ref):
    y = at_ref[0]
    for half, ref in ((y, mine_ref), (1 - y, theirs_ref)):
        for j in range(8):
            slab = ref[j].astype(jnp.float32)
            first = pl.multiple_of(176 * j + 88 * half, 8)
            for g in range(11):
                wide_ref[pl.ds(first + 8 * g, 8), :] = slab[:, 264 * g : 264 * (g + 1)]
    out_ref[...] = wide_ref[...].astype(jnp.bfloat16)


def temporal_kernel(at_ref, same_ref, cross_ref, w_ref, out_ref, all_ref):
    assemble(at_ref, same_ref, cross_ref, all_ref)
    own = jnp.concatenate([all_ref[j][:, :176] for j in range(8)], axis=1)
    other = jnp.concatenate([all_ref[j][:, 176:] for j in range(8)], axis=1)
    mixed = jnp.concatenate([own, other], axis=0)
    packed = jnp.dot(normalize(mixed), w_ref[...], preferred_element_type=jnp.float32).astype(jnp.bfloat16)
    n = packed.shape[0]
    row = lax.broadcasted_iota(jnp.int32, (n, n), 0) % 16
    col = lax.broadcasted_iota(jnp.int32, (n, n), 1) % 16
    out_ref[...] = fold(masked_attention(packed, row == col))


def result_kernel(at_ref, same_ref, cross_ref, mixed_ref, own_ref, other_ref, out_ref, all_ref):
    y = at_ref[0]
    assemble(at_ref, same_ref, cross_ref, all_ref)
    update = jnp.dot(heads_of(all_ref), columns(y, own_ref, other_ref), preferred_element_type=jnp.float32)
    for half in range(2):
        for j in range(8):
            frame = 4 * (j // 2) + 2 * (y if half == 0 else 1 - y) + j % 2
            residual = mixed_ref[16 * j : 16 * j + 16, 176 * half : 176 * (half + 1)].astype(jnp.float32)
            at = 128 * half + 16 * j
            out_ref[frame] = (residual + update[at : at + 16]).astype(jnp.bfloat16)


def finish_kernel(blocks_ref, out_ref):
    for i in range(16):
        z, y, k = i // 4, (i // 2) % 2, i % 2
        block = blocks_ref[i]
        for other in range(2):
            at = 88 * (4 * z + 2 * other + k)
            out_ref[16 * y : 16 * y + 16, at : at + 88] = block[:, 88 * other : 88 * (other + 1)]


VM = pl.BlockSpec(memory_space=pltpu.VMEM)
SM = pl.BlockSpec(memory_space=pltpu.SMEM)


def kernel_call(body, shapes, n_in, scratch=(), scalar=False):
    return pl.pallas_call(
        body,
        out_shape=shapes,
        in_specs=([SM] if scalar else []) + [VM] * n_in,
        out_specs=jax.tree.map(lambda _: VM, shapes),
        scratch_shapes=scratch,
        compiler_params=pltpu.CompilerParams(vmem_limit_bytes=40 * 1024 * 1024),
    )


def to(mask):
    return [(i, i ^ mask) for i in range(16)]


def head_body(video, spatial_qkv, spatial_out, temporal_qkv, temporal_out):
    _, patches, D = video.shape
    bf = jnp.bfloat16
    place = lax.axis_index("seq")
    at = jnp.stack([(place // 2) % 2, place // 4, place % 2])
    scatter = lambda a: lax.all_to_all(a, "seq", 0, 0, tiled=True, axis_index_groups=COLUMNS)
    across = lambda a: lax.ppermute(a, "seq", ACROSS_Y)

    def gather(a):
        far, mid, near = (lax.ppermute(a, "seq", to(m)) for m in (12, 8, 4))
        same = jnp.stack([a, near, mid, far])
        return same, lax.ppermute(same, "seq", to(1))

    def call(body, shapes, *args, scratch=()):
        return kernel_call(body, shapes, len(args), list(scratch), True)(at, *args)

    S = lambda *shape: jax.ShapeDtypeStruct(shape, bf)
    wide = pltpu.VMEM((D, 264), jnp.float32)
    heads = pltpu.VMEM((8, 64, 352), bf)

    so, to_ = spatial_out, temporal_out
    packed_one, frame = lax.optimization_barrier((pack_call(spatial_qkv), video.reshape(patches, D)))
    one = scatter(packed_one)
    tokens = gather(frame)
    so_o, to_o = across(so), across(to_)
    normed, picked = call(tokens_kernel, (S(256, D), S(256, 176)), *tokens, scratch=[pltpu.VMEM((8, patches, D), bf)])
    one, so_o, to_o, normed, two_r = lax.optimization_barrier((one, so_o, to_o, normed, temporal_qkv))
    one_o = across(one)
    two_w = scatter(pack_call(two_r))
    spatial = call(spatial_kernel, S(64, 352), normed, one, one_o, scratch=[wide])
    same, cross = gather(spatial)
    same, two_w = lax.optimization_barrier((same, two_w))
    two_o = across(two_w)
    keep, send = call(mixed_kernel, (S(128, 176), S(128, 176)), same, cross, picked, so, so_o, scratch=[heads])
    mixed = jnp.concatenate([keep, across(send)], axis=1)
    rows = call(rows_kernel, S(D, 264), two_w, two_o, scratch=[wide])
    temporal = call(
        temporal_kernel, S(64, 352), *gather(mixed), rows, scratch=[pltpu.VMEM((8, 128, 352), bf)]
    )
    result = call(result_kernel, S(16, 16, 176), *gather(temporal), mixed, to_, to_o, scratch=[heads])
    result = lax.all_to_all(result, "seq", 0, 0, tiled=True)
    return kernel_call(finish_kernel, S(patches, D), 1)(result).reshape(1, patches, D)


def solution(mesh):
    in_specs = (
        P(("groups", "seq"), None, None),
        P("seq", None),
        P(None, "seq"),
        P("seq", None),
        P(None, "seq"),
    )
    out_specs = P(("groups", "seq"), None, None)
    body = head_body if mesh.shape["seq"] == 16 else gathered_weights_body
    return jax.shard_map(body, mesh=mesh, in_specs=in_specs, out_specs=out_specs, check_vma=False)
```

```python
import jax
import jax.numpy as jnp
from jax import lax
from jax.experimental import pallas as pl
from jax.experimental.pallas import tpu as pltpu
from jax.sharding import PartitionSpec as P

HEADS = 8
HEAD_DIM = 88


def normalize(tokens):
    values = tokens.astype(jnp.float32)
    center = values - jnp.mean(values, axis=-1, keepdims=True)
    variance = jnp.mean(center * center, axis=-1, keepdims=True)
    return (center * lax.rsqrt(variance + 1e-06)).astype(jnp.bfloat16)


def attend(queries, keys_in, values_in):
    scores = jnp.einsum(
        "bqhe,bkhe->bhqk", queries, keys_in, preferred_element_type=jnp.float32
    ) * HEAD_DIM ** (-0.5)
    weights = jax.nn.softmax(scores, axis=-1).astype(jnp.bfloat16)
    return jnp.einsum(
        "bhqk,bkhe->bqhe", weights, values_in, preferred_element_type=jnp.float32
    ).astype(jnp.bfloat16)


def gathered_weights_body(video, spatial_qkv, spatial_out, temporal_qkv, temporal_out):
    frames, patches, model_width = video.shape
    head_total = HEADS * HEAD_DIM
    flat = video.reshape(-1, model_width)
    normed = normalize(flat)
    gathered = (
        lax.all_gather(spatial_qkv, "seq", axis=0, tiled=True),
        lax.all_gather(spatial_out, "seq", axis=1, tiled=True),
        lax.all_gather(temporal_qkv, "seq", axis=0, tiled=True),
        lax.all_gather(temporal_out, "seq", axis=1, tiled=True),
    )
    packed = (
        jnp.dot(normed, gathered[0], preferred_element_type=jnp.float32)
        .astype(jnp.bfloat16)
        .reshape(frames, patches, 3, HEADS, HEAD_DIM)
    )
    spatial = attend(packed[:, :, 0], packed[:, :, 1], packed[:, :, 2]).reshape(-1, head_total)
    mixed = (
        flat.astype(jnp.float32) + jnp.dot(spatial, gathered[1], preferred_element_type=jnp.float32)
    ).astype(jnp.bfloat16)
    mixed = mixed.reshape(frames, patches, model_width)
    moved = lax.all_to_all(mixed, "seq", split_axis=1, concat_axis=0, tiled=True)
    all_frames, local_patches = (moved.shape[0], moved.shape[1])
    normed_two = normalize(moved.reshape(-1, model_width))
    packed_two = jnp.dot(normed_two, gathered[2], preferred_element_type=jnp.float32).astype(
        jnp.bfloat16
    )
    packed_two = packed_two.reshape(all_frames, local_patches, 3, HEADS, HEAD_DIM).transpose(
        1, 0, 2, 3, 4
    )
    temporal = attend(packed_two[:, :, 0], packed_two[:, :, 1], packed_two[:, :, 2])
    temporal = temporal.transpose(1, 0, 2, 3).reshape(all_frames, local_patches, head_total)
    update = jnp.dot(
        temporal.reshape(-1, head_total), gathered[3], preferred_element_type=jnp.float32
    ).reshape(all_frames, local_patches, model_width)
    finished = (moved.astype(jnp.float32) + update).astype(jnp.bfloat16)
    return lax.all_to_all(finished, "seq", split_axis=0, concat_axis=1, tiled=True)


COLUMNS = [[4 * z + 2 * y + k for z in range(4) for k in range(2)] for y in range(2)]
ACROSS_Y = [(i, i ^ 2) for i in range(16)]


def pack(w):
    w = w.reshape(11, 8, 3, HEADS, HEAD_DIM)
    return w.transpose(3, 1, 0, 2, 4).reshape(HEADS, 8, 11 * 3 * HEAD_DIM)


def pack_kernel(w_ref, out_ref):
    for g in range(11):
        rows = w_ref[8 * g : 8 * (g + 1), :].astype(jnp.float32)
        for h in range(HEADS):
            for c in range(3):
                at = 264 * g + 88 * c
                piece = rows[:, 704 * c + 88 * h : 704 * c + 88 * (h + 1)]
                out_ref[h, :, at : at + 88] = piece.astype(jnp.bfloat16)


def pack_near_kernel(at_ref, w_ref, own_ref, near_ref, mid_ref, far_ref, all_ref):
    z, k = at_ref[1], at_ref[2]
    for g in range(11):
        rows = w_ref[8 * g : 8 * (g + 1), :].astype(jnp.float32)
        for h in range(HEADS):
            for c in range(3):
                at = 264 * g + 88 * c
                piece = rows[:, 704 * c + 88 * h : 704 * c + 88 * (h + 1)]
                all_ref[(h // 2) ^ z, (h % 2) ^ k, :, at : at + 88] = piece.astype(jnp.bfloat16)
    for d, ref in enumerate((own_ref, near_ref, mid_ref, far_ref)):
        ref[...] = all_ref[d]


def pack_call(w):
    return kernel_call(pack_kernel, jax.ShapeDtypeStruct((HEADS, 8, 11 * 264), jnp.bfloat16), 1)(w)


def unpack(at_ref, pieces, wide_ref):
    y, z, k = at_ref[0], at_ref[1], at_ref[2]
    for dz, dy, dk, piece in pieces:
        slab = piece.astype(jnp.float32)
        first = pl.multiple_of(88 * (4 * (z ^ dz) + 2 * (y ^ dy) + (k ^ dk)), 8)
        for g in range(11):
            wide_ref[pl.ds(first + 8 * g, 8), :] = slab[:, 264 * g : 264 * (g + 1)]
    return wide_ref[...].astype(jnp.bfloat16)


def masked_attention(packed, same):
    q, k, v = packed[:, :88], packed[:, 88:176], packed[:, 176:]
    scores = lax.dot_general(q, k, (((1,), (1,)), ((), ())), preferred_element_type=jnp.float32) * HEAD_DIM ** (-0.5)
    scores = jnp.where(same, scores, -jnp.inf)
    top = jnp.max(scores, axis=-1, keepdims=True)
    e = jnp.exp(scores - top)
    weights = (e / jnp.sum(e, axis=-1, keepdims=True)).astype(jnp.bfloat16)
    return jnp.dot(weights, v, preferred_element_type=jnp.float32).astype(jnp.bfloat16)


def assemble(at_ref, same_ref, cross_ref, all_ref):
    z, k = at_ref[1], at_ref[2]
    for d in range(4):
        first = 2 * (z ^ d)
        all_ref[first + k] = same_ref[d]
        all_ref[first + 1 - k] = cross_ref[d]


def heads_of(all_ref):
    parts = []
    for r in range(4):
        parts.append(jnp.concatenate([all_ref[h][:, 88 * r : 88 * (r + 1)] for h in range(HEADS)], axis=1))
    return jnp.concatenate(parts, axis=0)


def fold(rows):
    return jnp.concatenate([rows[64 * r : 64 * (r + 1)] for r in range(4)], axis=1)


def tokens_kernel(at_ref, same_ref, cross_ref, normed_ref, picked_ref, all_ref):
    assemble(at_ref, same_ref, cross_ref, all_ref)
    y, z, k = at_ref[0], at_ref[1], at_ref[2]
    n = all_ref.shape[2]
    row = lax.broadcasted_iota(jnp.int32, (n, 176), 0)
    col = lax.broadcasted_iota(jnp.int32, (n, 176), 1)
    first = 88 * (4 * z + k)
    place = jnp.where(col < 88, first + col, first + 88 + col)
    chosen = (row == place).astype(jnp.float32).astype(jnp.bfloat16)
    tokens = jnp.concatenate([all_ref[j] for j in range(8)], axis=0)
    normed_ref[...] = normalize(tokens)
    picked_ref[...] = jnp.dot(tokens, chosen, preferred_element_type=jnp.float32).astype(jnp.bfloat16)


def spatial_kernel(at_ref, normed_ref, same_ref, cross_ref, same_y_ref, cross_y_ref, out_ref, wide_ref):
    pieces = []
    for dy, same, cross in ((0, same_ref, cross_ref), (1, same_y_ref, cross_y_ref)):
        for d in range(4):
            pieces += [(d, dy, 0, same[d, 0]), (d, dy, 1, cross[d])]
    w = unpack(at_ref, pieces, wide_ref)
    packed = jnp.dot(normed_ref[...], w, preferred_element_type=jnp.float32).astype(jnp.bfloat16)
    n = packed.shape[0]
    row = lax.broadcasted_iota(jnp.int32, (n, n), 0) // 32
    col = lax.broadcasted_iota(jnp.int32, (n, n), 1) // 32
    out_ref[...] = fold(masked_attention(packed, row == col))


def project(y, heads, own_ref, other_ref):
    own, other = (
        lax.dot_general(heads, ref[...], (((1,), (1,)), ((), ())), preferred_element_type=jnp.float32) for ref in (own_ref, other_ref)
    )
    return jnp.concatenate([jnp.where(y == 0, own, other), jnp.where(y == 0, other, own)], axis=1)


def mixed_kernel(at_ref, same_ref, cross_ref, picked_ref, own_ref, other_ref, keep_ref, send_ref, all_ref):
    y = at_ref[0]
    assemble(at_ref, same_ref, cross_ref, all_ref)
    update = project(y, heads_of(all_ref), own_ref, other_ref)
    mixed = picked_ref[...].astype(jnp.float32) + update
    for j in range(8):
        low, high = mixed[32 * j : 32 * j + 16], mixed[32 * j + 16 : 32 * j + 32]
        keep_ref[16 * j : 16 * j + 16, :] = jnp.where(y == 0, low, high).astype(jnp.bfloat16)
        send_ref[16 * j : 16 * j + 16, :] = jnp.where(y == 0, high, low).astype(jnp.bfloat16)


def rows_kernel(at_ref, mine_ref, theirs_ref, out_ref, wide_ref):
    y = at_ref[0]
    for half, ref in ((y, mine_ref), (1 - y, theirs_ref)):
        for j in range(8):
            slab = ref[j].astype(jnp.float32)
            first = pl.multiple_of(176 * j + 88 * half, 8)
            for g in range(11):
                wide_ref[pl.ds(first + 8 * g, 8), :] = slab[:, 264 * g : 264 * (g + 1)]
    out_ref[...] = wide_ref[...].astype(jnp.bfloat16)


def temporal_kernel(at_ref, same_ref, cross_ref, w_ref, out_ref, all_ref):
    assemble(at_ref, same_ref, cross_ref, all_ref)
    own = jnp.concatenate([all_ref[j][:, :176] for j in range(8)], axis=1)
    other = jnp.concatenate([all_ref[j][:, 176:] for j in range(8)], axis=1)
    mixed = jnp.concatenate([own, other], axis=0)
    packed = jnp.dot(normalize(mixed), w_ref[...], preferred_element_type=jnp.float32).astype(jnp.bfloat16)
    n = packed.shape[0]
    row = lax.broadcasted_iota(jnp.int32, (n, n), 0) % 16
    col = lax.broadcasted_iota(jnp.int32, (n, n), 1) % 16
    out_ref[...] = fold(masked_attention(packed, row == col))


def result_kernel(at_ref, same_ref, cross_ref, mixed_ref, own_ref, other_ref, out_ref, all_ref):
    y = at_ref[0]
    assemble(at_ref, same_ref, cross_ref, all_ref)
    update = project(y, heads_of(all_ref), own_ref, other_ref)
    for half in range(2):
        for j in range(8):
            frame = 4 * (j // 2) + 2 * (y if half == 0 else 1 - y) + j % 2
            residual = mixed_ref[16 * j : 16 * j + 16, 176 * half : 176 * (half + 1)].astype(jnp.float32)
            at = 128 * half + 16 * j
            rows = (residual + update[at : at + 16]).astype(jnp.bfloat16)
            out_ref[frame] = jnp.concatenate([rows[:8], rows[8:]], axis=1)


def finish_kernel(blocks_ref, out_ref):
    for i in range(16):
        z, y, k = i // 4, (i // 2) % 2, i % 2
        block = blocks_ref[i]
        for other in range(2):
            at = 88 * (4 * z + 2 * other + k)
            for half in range(2):
                first = 16 * y + 8 * half
                out_ref[first : first + 8, at : at + 88] = block[:, 176 * half + 88 * other : 176 * half + 88 * (other + 1)]


VM = pl.BlockSpec(memory_space=pltpu.VMEM)
SM = pl.BlockSpec(memory_space=pltpu.SMEM)


def kernel_call(body, shapes, n_in, scratch=(), scalar=False):
    return pl.pallas_call(
        body,
        out_shape=shapes,
        in_specs=([SM] if scalar else []) + [VM] * n_in,
        out_specs=jax.tree.map(lambda _: VM, shapes),
        scratch_shapes=scratch,
        compiler_params=pltpu.CompilerParams(vmem_limit_bytes=40 * 1024 * 1024),
    )


def to(mask):
    return [(i, i ^ mask) for i in range(16)]


def head_body(video, spatial_qkv, spatial_out, temporal_qkv, temporal_out):
    _, patches, D = video.shape
    bf = jnp.bfloat16
    place = lax.axis_index("seq")
    at = jnp.stack([(place // 2) % 2, place // 4, place % 2])
    scatter = lambda a: lax.all_to_all(a, "seq", 0, 0, tiled=True, axis_index_groups=COLUMNS)
    across = lambda a: lax.ppermute(a, "seq", ACROSS_Y)

    def gather(a):
        far, mid, near = (lax.ppermute(a, "seq", to(m)) for m in (12, 8, 4))
        same = jnp.stack([a, near, mid, far])
        return same, lax.ppermute(same, "seq", to(1))

    def call(body, shapes, *args, scratch=()):
        return kernel_call(body, shapes, len(args), list(scratch), True)(at, *args)

    S = lambda *shape: jax.ShapeDtypeStruct(shape, bf)
    wide = pltpu.VMEM((D, 264), jnp.float32)
    heads = pltpu.VMEM((8, 64, 352), bf)

    so, to_ = spatial_out.T, temporal_out.T
    part = S(2, 8, 11 * 264)
    parts = call(pack_near_kernel, (part,) * 4, spatial_qkv, scratch=[pltpu.VMEM((4, 2, 8, 11 * 264), bf)])
    near, mid, far = (lax.ppermute(p, "seq", to(m)) for p, m in zip(parts[1:], (4, 8, 12)))
    so_o, to_o = across(so), across(to_)
    near, mid, far, so_o, to_o, frame, packed_two = lax.optimization_barrier(
        (near, mid, far, so_o, to_o, video.reshape(patches, D), pack_call(temporal_qkv))
    )
    all_w = jnp.stack([parts[0], near, mid, far])
    all_y = across(all_w)
    cross_w = lax.ppermute(all_w[:, 1], "seq", to(1))
    two_w = scatter(packed_two)
    t_far, t_mid, t_near = (lax.ppermute(frame, "seq", to(m)) for m in (12, 8, 4))
    same = jnp.stack([frame, t_near, t_mid, t_far])
    same, all_y = lax.optimization_barrier((same, all_y))
    tokens = same, lax.ppermute(same, "seq", to(1))
    cross_y = lax.ppermute(all_y[:, 1], "seq", to(1))
    normed, picked = call(tokens_kernel, (S(256, D), S(256, 176)), *tokens, scratch=[pltpu.VMEM((8, patches, D), bf)])
    spatial = call(spatial_kernel, S(64, 352), normed, all_w, cross_w, all_y, cross_y, scratch=[wide])
    same, cross = gather(spatial)
    same, two_w = lax.optimization_barrier((same, two_w))
    two_o = across(two_w)
    keep, send = call(mixed_kernel, (S(128, 176), S(128, 176)), same, cross, picked, so, so_o, scratch=[heads])
    mixed = jnp.concatenate([keep, across(send)], axis=1)
    rows = call(rows_kernel, S(D, 264), two_w, two_o, scratch=[wide])
    temporal = call(
        temporal_kernel, S(64, 352), *gather(mixed), rows, scratch=[pltpu.VMEM((8, 128, 352), bf)]
    )
    result = call(result_kernel, S(16, 8, 352), *gather(temporal), mixed, to_, to_o, scratch=[heads])
    result = lax.all_to_all(result, "seq", 0, 0, tiled=True)
    return kernel_call(finish_kernel, S(patches, D), 1)(result).reshape(1, patches, D)


def solution(mesh):
    in_specs = (
        P(("groups", "seq"), None, None),
        P("seq", None),
        P(None, "seq"),
        P("seq", None),
        P(None, "seq"),
    )
    out_specs = P(("groups", "seq"), None, None)
    body = head_body if mesh.shape["seq"] == 16 else gathered_weights_body
    return jax.shard_map(body, mesh=mesh, in_specs=in_specs, out_specs=out_specs, check_vma=False)
```

```python
import jax
import jax.numpy as jnp
from jax import lax
from jax.experimental import pallas as pl
from jax.experimental.pallas import tpu as pltpu
from jax.sharding import PartitionSpec as P

HEADS = 8
HEAD_DIM = 88


def normalize(tokens):
    values = tokens.astype(jnp.float32)
    center = values - jnp.mean(values, axis=-1, keepdims=True)
    variance = jnp.mean(center * center, axis=-1, keepdims=True)
    return (center * lax.rsqrt(variance + 1e-06)).astype(jnp.bfloat16)


def attend(queries, keys_in, values_in):
    scores = jnp.einsum(
        "bqhe,bkhe->bhqk", queries, keys_in, preferred_element_type=jnp.float32
    ) * HEAD_DIM ** (-0.5)
    weights = jax.nn.softmax(scores, axis=-1).astype(jnp.bfloat16)
    return jnp.einsum(
        "bhqk,bkhe->bqhe", weights, values_in, preferred_element_type=jnp.float32
    ).astype(jnp.bfloat16)


def gathered_weights_body(video, spatial_qkv, spatial_out, temporal_qkv, temporal_out):
    frames, patches, model_width = video.shape
    head_total = HEADS * HEAD_DIM
    flat = video.reshape(-1, model_width)
    normed = normalize(flat)
    gathered = (
        lax.all_gather(spatial_qkv, "seq", axis=0, tiled=True),
        lax.all_gather(spatial_out, "seq", axis=1, tiled=True),
        lax.all_gather(temporal_qkv, "seq", axis=0, tiled=True),
        lax.all_gather(temporal_out, "seq", axis=1, tiled=True),
    )
    packed = (
        jnp.dot(normed, gathered[0], preferred_element_type=jnp.float32)
        .astype(jnp.bfloat16)
        .reshape(frames, patches, 3, HEADS, HEAD_DIM)
    )
    spatial = attend(packed[:, :, 0], packed[:, :, 1], packed[:, :, 2]).reshape(-1, head_total)
    mixed = (
        flat.astype(jnp.float32) + jnp.dot(spatial, gathered[1], preferred_element_type=jnp.float32)
    ).astype(jnp.bfloat16)
    mixed = mixed.reshape(frames, patches, model_width)
    moved = lax.all_to_all(mixed, "seq", split_axis=1, concat_axis=0, tiled=True)
    all_frames, local_patches = (moved.shape[0], moved.shape[1])
    normed_two = normalize(moved.reshape(-1, model_width))
    packed_two = jnp.dot(normed_two, gathered[2], preferred_element_type=jnp.float32).astype(
        jnp.bfloat16
    )
    packed_two = packed_two.reshape(all_frames, local_patches, 3, HEADS, HEAD_DIM).transpose(
        1, 0, 2, 3, 4
    )
    temporal = attend(packed_two[:, :, 0], packed_two[:, :, 1], packed_two[:, :, 2])
    temporal = temporal.transpose(1, 0, 2, 3).reshape(all_frames, local_patches, head_total)
    update = jnp.dot(
        temporal.reshape(-1, head_total), gathered[3], preferred_element_type=jnp.float32
    ).reshape(all_frames, local_patches, model_width)
    finished = (moved.astype(jnp.float32) + update).astype(jnp.bfloat16)
    return lax.all_to_all(finished, "seq", split_axis=0, concat_axis=1, tiled=True)


COLUMNS = [[4 * z + 2 * y + k for z in range(4) for k in range(2)] for y in range(2)]
ACROSS_Y = [(i, i ^ 2) for i in range(16)]


def pack(w):
    w = w.reshape(11, 8, 3, HEADS, HEAD_DIM)
    return w.transpose(3, 1, 0, 2, 4).reshape(HEADS, 8, 11 * 3 * HEAD_DIM)


def pack_kernel(w_ref, out_ref):
    for g in range(11):
        rows = w_ref[8 * g : 8 * (g + 1), :].astype(jnp.float32)
        for h in range(HEADS):
            for c in range(3):
                at = 264 * g + 88 * c
                piece = rows[:, 704 * c + 88 * h : 704 * c + 88 * (h + 1)]
                out_ref[h, :, at : at + 88] = piece.astype(jnp.bfloat16)


def pack_near_kernel(at_ref, w_ref, own_ref, near_ref, mid_ref, far_ref, all_ref):
    z, k = at_ref[1], at_ref[2]
    for g in range(11):
        rows = w_ref[8 * g : 8 * (g + 1), :].astype(jnp.float32)
        for h in range(HEADS):
            for c in range(3):
                at = 264 * g + 88 * c
                piece = rows[:, 704 * c + 88 * h : 704 * c + 88 * (h + 1)]
                all_ref[(h // 2) ^ z, (h % 2) ^ k, :, at : at + 88] = piece.astype(jnp.bfloat16)
    for d, ref in enumerate((own_ref, near_ref, mid_ref, far_ref)):
        ref[...] = all_ref[d]


def pack_call(w):
    return kernel_call(pack_kernel, jax.ShapeDtypeStruct((HEADS, 8, 11 * 264), jnp.bfloat16), 1)(w)


def unpack(at_ref, pieces, wide_ref):
    y, z, k = at_ref[0], at_ref[1], at_ref[2]
    for dz, dy, dk, piece in pieces:
        slab = piece.astype(jnp.float32)
        first = pl.multiple_of(88 * (4 * (z ^ dz) + 2 * (y ^ dy) + (k ^ dk)), 8)
        for g in range(11):
            wide_ref[pl.ds(first + 8 * g, 8), :] = slab[:, 264 * g : 264 * (g + 1)]
    return wide_ref[...].astype(jnp.bfloat16)


def masked_attention(packed, same):
    q, k, v = packed[:, :88], packed[:, 88:176], packed[:, 176:]
    scores = lax.dot_general(q, k, (((1,), (1,)), ((), ())), preferred_element_type=jnp.float32) * HEAD_DIM ** (-0.5)
    scores = jnp.where(same, scores, -jnp.inf)
    top = jnp.max(scores, axis=-1, keepdims=True)
    e = jnp.exp(scores - top)
    weights = (e / jnp.sum(e, axis=-1, keepdims=True)).astype(jnp.bfloat16)
    return jnp.dot(weights, v, preferred_element_type=jnp.float32).astype(jnp.bfloat16)


def assemble(at_ref, same_ref, cross_ref, all_ref):
    z, k = at_ref[1], at_ref[2]
    for d in range(4):
        first = 2 * (z ^ d)
        all_ref[first + k] = same_ref[d]
        all_ref[first + 1 - k] = cross_ref[d]


def heads_of(all_ref):
    parts = []
    for r in range(4):
        parts.append(jnp.concatenate([all_ref[h][:, 88 * r : 88 * (r + 1)] for h in range(HEADS)], axis=1))
    return jnp.concatenate(parts, axis=0)


def fold(rows):
    return jnp.concatenate([rows[64 * r : 64 * (r + 1)] for r in range(4)], axis=1)


def tokens_kernel(at_ref, same_ref, cross_ref, normed_ref, picked_ref, all_ref):
    assemble(at_ref, same_ref, cross_ref, all_ref)
    y, z, k = at_ref[0], at_ref[1], at_ref[2]
    n = all_ref.shape[2]
    row = lax.broadcasted_iota(jnp.int32, (n, 176), 0)
    col = lax.broadcasted_iota(jnp.int32, (n, 176), 1)
    first = 88 * (4 * z + k)
    place = jnp.where(col < 88, first + col, first + 88 + col)
    chosen = (row == place).astype(jnp.float32).astype(jnp.bfloat16)
    tokens = jnp.concatenate([all_ref[j] for j in range(8)], axis=0)
    normed_ref[...] = normalize(tokens)
    picked_ref[...] = jnp.dot(tokens, chosen, preferred_element_type=jnp.float32).astype(jnp.bfloat16)


def spatial_kernel(at_ref, tokens_same_ref, tokens_cross_ref, same_ref, cross_ref, same_y_ref, cross_y_ref, out_ref, picked_ref, wide_ref, normed_ref, all_ref):
    tokens_kernel(at_ref, tokens_same_ref, tokens_cross_ref, normed_ref, picked_ref, all_ref)
    pieces = []
    for dy, same, cross in ((0, same_ref, cross_ref), (1, same_y_ref, cross_y_ref)):
        for d in range(4):
            pieces += [(d, dy, 0, same[d, 0]), (d, dy, 1, cross[d])]
    w = unpack(at_ref, pieces, wide_ref)
    packed = jnp.dot(normed_ref[...], w, preferred_element_type=jnp.float32).astype(jnp.bfloat16)
    n = packed.shape[0]
    row = lax.broadcasted_iota(jnp.int32, (n, n), 0) // 32
    col = lax.broadcasted_iota(jnp.int32, (n, n), 1) // 32
    out_ref[...] = fold(masked_attention(packed, row == col))


def project(y, heads, own_ref, other_ref):
    own, other = (
        lax.dot_general(heads, ref[...], (((1,), (1,)), ((), ())), preferred_element_type=jnp.float32) for ref in (own_ref, other_ref)
    )
    return jnp.concatenate([jnp.where(y == 0, own, other), jnp.where(y == 0, other, own)], axis=1)


def mixed_kernel(at_ref, same_ref, cross_ref, picked_ref, own_ref, other_ref, keep_ref, send_ref, all_ref):
    y = at_ref[0]
    assemble(at_ref, same_ref, cross_ref, all_ref)
    update = project(y, heads_of(all_ref), own_ref, other_ref)
    mixed = picked_ref[...].astype(jnp.float32) + update
    for j in range(8):
        low, high = mixed[32 * j : 32 * j + 16], mixed[32 * j + 16 : 32 * j + 32]
        keep_ref[16 * j : 16 * j + 16, :] = jnp.where(y == 0, low, high).astype(jnp.bfloat16)
        send_ref[16 * j : 16 * j + 16, :] = jnp.where(y == 0, high, low).astype(jnp.bfloat16)


def rows_kernel(at_ref, mine_ref, theirs_ref, out_ref, wide_ref):
    y = at_ref[0]
    for half, ref in ((y, mine_ref), (1 - y, theirs_ref)):
        for j in range(8):
            slab = ref[j].astype(jnp.float32)
            first = pl.multiple_of(176 * j + 88 * half, 8)
            for g in range(11):
                wide_ref[pl.ds(first + 8 * g, 8), :] = slab[:, 264 * g : 264 * (g + 1)]
    out_ref[...] = wide_ref[...].astype(jnp.bfloat16)


def temporal_kernel(at_ref, same_ref, cross_ref, w_ref, out_ref, all_ref):
    assemble(at_ref, same_ref, cross_ref, all_ref)
    own = jnp.concatenate([all_ref[j][:, :176] for j in range(8)], axis=1)
    other = jnp.concatenate([all_ref[j][:, 176:] for j in range(8)], axis=1)
    mixed = jnp.concatenate([own, other], axis=0)
    packed = jnp.dot(normalize(mixed), w_ref[...], preferred_element_type=jnp.float32).astype(jnp.bfloat16)
    n = packed.shape[0]
    row = lax.broadcasted_iota(jnp.int32, (n, n), 0) % 16
    col = lax.broadcasted_iota(jnp.int32, (n, n), 1) % 16
    out_ref[...] = fold(masked_attention(packed, row == col))


def result_kernel(at_ref, same_ref, cross_ref, mixed_ref, own_ref, other_ref, out_ref, all_ref):
    y = at_ref[0]
    assemble(at_ref, same_ref, cross_ref, all_ref)
    update = project(y, heads_of(all_ref), own_ref, other_ref)
    for half in range(2):
        for j in range(8):
            frame = 4 * (j // 2) + 2 * (y if half == 0 else 1 - y) + j % 2
            residual = mixed_ref[16 * j : 16 * j + 16, 176 * half : 176 * (half + 1)].astype(jnp.float32)
            at = 128 * half + 16 * j
            rows = (residual + update[at : at + 16]).astype(jnp.bfloat16)
            out_ref[frame] = jnp.concatenate([rows[:8], rows[8:]], axis=1)


def finish_kernel(blocks_ref, out_ref):
    for i in range(16):
        z, y, k = i // 4, (i // 2) % 2, i % 2
        block = blocks_ref[i]
        for other in range(2):
            at = 88 * (4 * z + 2 * other + k)
            for half in range(2):
                first = 16 * y + 8 * half
                out_ref[first : first + 8, at : at + 88] = block[:, 176 * half + 88 * other : 176 * half + 88 * (other + 1)]


VM = pl.BlockSpec(memory_space=pltpu.VMEM)
SM = pl.BlockSpec(memory_space=pltpu.SMEM)


def kernel_call(body, shapes, n_in, scratch=(), scalar=False):
    return pl.pallas_call(
        body,
        out_shape=shapes,
        in_specs=([SM] if scalar else []) + [VM] * n_in,
        out_specs=jax.tree.map(lambda _: VM, shapes),
        scratch_shapes=scratch,
        compiler_params=pltpu.CompilerParams(vmem_limit_bytes=40 * 1024 * 1024),
    )


def to(mask):
    return [(i, i ^ mask) for i in range(16)]


def head_body(video, spatial_qkv, spatial_out, temporal_qkv, temporal_out):
    _, patches, D = video.shape
    bf = jnp.bfloat16
    place = lax.axis_index("seq")
    at = jnp.stack([(place // 2) % 2, place // 4, place % 2])
    scatter = lambda a: lax.all_to_all(a, "seq", 0, 0, tiled=True, axis_index_groups=COLUMNS)
    across = lambda a: lax.ppermute(a, "seq", ACROSS_Y)

    def gather(a):
        far, mid, near = (lax.ppermute(a, "seq", to(m)) for m in (12, 8, 4))
        same = jnp.stack([a, near, mid, far])
        return same, lax.ppermute(same, "seq", to(1))

    def call(body, shapes, *args, scratch=()):
        return kernel_call(body, shapes, len(args), list(scratch), True)(at, *args)

    S = lambda *shape: jax.ShapeDtypeStruct(shape, bf)
    wide = pltpu.VMEM((D, 264), jnp.float32)
    heads = pltpu.VMEM((8, 64, 352), bf)

    so, to_ = spatial_out.T, temporal_out.T
    part = S(2, 8, 11 * 264)
    parts = call(pack_near_kernel, (part,) * 4, spatial_qkv, scratch=[pltpu.VMEM((4, 2, 8, 11 * 264), bf)])
    near, mid, far = (lax.ppermute(p, "seq", to(m)) for p, m in zip(parts[1:], (4, 8, 12)))
    so_o, to_o = across(so), across(to_)
    near, mid, far, so_o, to_o, frame, packed_two = lax.optimization_barrier(
        (near, mid, far, so_o, to_o, video.reshape(patches, D), pack_call(temporal_qkv))
    )
    all_w = jnp.stack([parts[0], near, mid, far])
    all_y = across(all_w)
    cross_w = lax.ppermute(all_w[:, 1], "seq", to(1))
    two_w = scatter(packed_two)
    t_far, t_mid, t_near = (lax.ppermute(frame, "seq", to(m)) for m in (12, 8, 4))
    same = jnp.stack([frame, t_near, t_mid, t_far])
    same, all_y = lax.optimization_barrier((same, all_y))
    tokens = same, lax.ppermute(same, "seq", to(1))
    cross_y = lax.ppermute(all_y[:, 1], "seq", to(1))
    spatial, picked = call(
        spatial_kernel, (S(64, 352), S(256, 176)), *tokens, all_w, cross_w, all_y, cross_y,
        scratch=[wide, pltpu.VMEM((256, D), bf), pltpu.VMEM((8, patches, D), bf)],
    )
    same, cross = gather(spatial)
    same, two_w = lax.optimization_barrier((same, two_w))
    two_o = across(two_w)
    keep, send = call(mixed_kernel, (S(128, 176), S(128, 176)), same, cross, picked, so, so_o, scratch=[heads])
    mixed = jnp.concatenate([keep, across(send)], axis=1)
    rows = call(rows_kernel, S(D, 264), two_w, two_o, scratch=[wide])
    temporal = call(
        temporal_kernel, S(64, 352), *gather(mixed), rows, scratch=[pltpu.VMEM((8, 128, 352), bf)]
    )
    result = call(result_kernel, S(16, 8, 352), *gather(temporal), mixed, to_, to_o, scratch=[heads])
    result = lax.all_to_all(result, "seq", 0, 0, tiled=True)
    return kernel_call(finish_kernel, S(patches, D), 1)(result).reshape(1, patches, D)


def solution(mesh):
    in_specs = (
        P(("groups", "seq"), None, None),
        P("seq", None),
        P(None, "seq"),
        P("seq", None),
        P(None, "seq"),
    )
    out_specs = P(("groups", "seq"), None, None)
    body = head_body if mesh.shape["seq"] == 16 else gathered_weights_body
    return jax.shard_map(body, mesh=mesh, in_specs=in_specs, out_specs=out_specs, check_vma=False)
```

```python
import jax
import jax.numpy as jnp
from jax import lax
from jax.experimental import pallas as pl
from jax.experimental.pallas import tpu as pltpu
from jax.sharding import PartitionSpec as P

HEADS = 8
HEAD_DIM = 88


def normalize(tokens):
    values = tokens.astype(jnp.float32)
    center = values - jnp.mean(values, axis=-1, keepdims=True)
    variance = jnp.mean(center * center, axis=-1, keepdims=True)
    return (center * lax.rsqrt(variance + 1e-06)).astype(jnp.bfloat16)


def attend(queries, keys_in, values_in):
    scores = jnp.einsum(
        "bqhe,bkhe->bhqk", queries, keys_in, preferred_element_type=jnp.float32
    ) * HEAD_DIM ** (-0.5)
    weights = jax.nn.softmax(scores, axis=-1).astype(jnp.bfloat16)
    return jnp.einsum(
        "bhqk,bkhe->bqhe", weights, values_in, preferred_element_type=jnp.float32
    ).astype(jnp.bfloat16)


def gathered_weights_body(video, spatial_qkv, spatial_out, temporal_qkv, temporal_out):
    frames, patches, model_width = video.shape
    head_total = HEADS * HEAD_DIM
    flat = video.reshape(-1, model_width)
    normed = normalize(flat)
    gathered = (
        lax.all_gather(spatial_qkv, "seq", axis=0, tiled=True),
        lax.all_gather(spatial_out, "seq", axis=1, tiled=True),
        lax.all_gather(temporal_qkv, "seq", axis=0, tiled=True),
        lax.all_gather(temporal_out, "seq", axis=1, tiled=True),
    )
    packed = (
        jnp.dot(normed, gathered[0], preferred_element_type=jnp.float32)
        .astype(jnp.bfloat16)
        .reshape(frames, patches, 3, HEADS, HEAD_DIM)
    )
    spatial = attend(packed[:, :, 0], packed[:, :, 1], packed[:, :, 2]).reshape(-1, head_total)
    mixed = (
        flat.astype(jnp.float32) + jnp.dot(spatial, gathered[1], preferred_element_type=jnp.float32)
    ).astype(jnp.bfloat16)
    mixed = mixed.reshape(frames, patches, model_width)
    moved = lax.all_to_all(mixed, "seq", split_axis=1, concat_axis=0, tiled=True)
    all_frames, local_patches = (moved.shape[0], moved.shape[1])
    normed_two = normalize(moved.reshape(-1, model_width))
    packed_two = jnp.dot(normed_two, gathered[2], preferred_element_type=jnp.float32).astype(
        jnp.bfloat16
    )
    packed_two = packed_two.reshape(all_frames, local_patches, 3, HEADS, HEAD_DIM).transpose(
        1, 0, 2, 3, 4
    )
    temporal = attend(packed_two[:, :, 0], packed_two[:, :, 1], packed_two[:, :, 2])
    temporal = temporal.transpose(1, 0, 2, 3).reshape(all_frames, local_patches, head_total)
    update = jnp.dot(
        temporal.reshape(-1, head_total), gathered[3], preferred_element_type=jnp.float32
    ).reshape(all_frames, local_patches, model_width)
    finished = (moved.astype(jnp.float32) + update).astype(jnp.bfloat16)
    return lax.all_to_all(finished, "seq", split_axis=0, concat_axis=1, tiled=True)


COLUMNS = [[4 * z + 2 * y + k for z in range(4) for k in range(2)] for y in range(2)]
ACROSS_Y = [(i, i ^ 2) for i in range(16)]


def pack(w):
    w = w.reshape(11, 8, 3, HEADS, HEAD_DIM)
    return w.transpose(3, 1, 0, 2, 4).reshape(HEADS, 8, 11 * 3 * HEAD_DIM)


def pack_kernel(w_ref, out_ref):
    for g in range(11):
        rows = w_ref[8 * g : 8 * (g + 1), :].astype(jnp.float32)
        for h in range(HEADS):
            for c in range(3):
                at = 264 * g + 88 * c
                piece = rows[:, 704 * c + 88 * h : 704 * c + 88 * (h + 1)]
                out_ref[h, :, at : at + 88] = piece.astype(jnp.bfloat16)


def pack_near_kernel(at_ref, w_ref, own_ref, near_ref, mid_ref, far_ref, all_ref):
    z, k = at_ref[1], at_ref[2]
    for g in range(11):
        rows = w_ref[8 * g : 8 * (g + 1), :].astype(jnp.float32)
        for h in range(HEADS):
            for c in range(3):
                at = 264 * g + 88 * c
                piece = rows[:, 704 * c + 88 * h : 704 * c + 88 * (h + 1)]
                all_ref[(h // 2) ^ z, (h % 2) ^ k, :, at : at + 88] = piece.astype(jnp.bfloat16)
    for d, ref in enumerate((own_ref, near_ref, mid_ref, far_ref)):
        ref[...] = all_ref[d]


def pack_call(w):
    return kernel_call(pack_kernel, jax.ShapeDtypeStruct((HEADS, 8, 11 * 264), jnp.bfloat16), 1)(w)


def unpack(at_ref, pieces, wide_ref):
    y, z, k = at_ref[0], at_ref[1], at_ref[2]
    for dz, dy, dk, piece in pieces:
        slab = piece.astype(jnp.float32)
        first = pl.multiple_of(88 * (4 * (z ^ dz) + 2 * (y ^ dy) + (k ^ dk)), 8)
        for g in range(11):
            wide_ref[pl.ds(first + 8 * g, 8), :] = slab[:, 264 * g : 264 * (g + 1)]
    return wide_ref[...].astype(jnp.bfloat16)


def masked_attention(packed, same):
    q, k, v = packed[:, :88], packed[:, 88:176], packed[:, 176:]
    scores = lax.dot_general(q, k, (((1,), (1,)), ((), ())), preferred_element_type=jnp.float32) * HEAD_DIM ** (-0.5)
    scores = jnp.where(same, scores, -jnp.inf)
    top = jnp.max(scores, axis=-1, keepdims=True)
    e = jnp.exp(scores - top)
    weights = (e / jnp.sum(e, axis=-1, keepdims=True)).astype(jnp.bfloat16)
    return jnp.dot(weights, v, preferred_element_type=jnp.float32).astype(jnp.bfloat16)


def assemble(at_ref, same_ref, cross_ref, all_ref):
    z, k = at_ref[1], at_ref[2]
    for d in range(4):
        first = 2 * (z ^ d)
        all_ref[first + k] = same_ref[d]
        all_ref[first + 1 - k] = cross_ref[d]


def heads_of(all_ref):
    parts = []
    for r in range(4):
        parts.append(jnp.concatenate([all_ref[h][:, 88 * r : 88 * (r + 1)] for h in range(HEADS)], axis=1))
    return jnp.concatenate(parts, axis=0)


def fold(rows):
    return jnp.concatenate([rows[64 * r : 64 * (r + 1)] for r in range(4)], axis=1)


def tokens_kernel(at_ref, same_ref, cross_ref, normed_ref, picked_ref, all_ref):
    assemble(at_ref, same_ref, cross_ref, all_ref)
    y, z, k = at_ref[0], at_ref[1], at_ref[2]
    n = all_ref.shape[2]
    row = lax.broadcasted_iota(jnp.int32, (n, 176), 0)
    col = lax.broadcasted_iota(jnp.int32, (n, 176), 1)
    first = 88 * (4 * z + k)
    place = jnp.where(col < 88, first + col, first + 88 + col)
    chosen = (row == place).astype(jnp.float32).astype(jnp.bfloat16)
    tokens = jnp.concatenate([all_ref[j] for j in range(8)], axis=0)
    normed_ref[...] = normalize(tokens)
    picked_ref[...] = jnp.dot(tokens, chosen, preferred_element_type=jnp.float32).astype(jnp.bfloat16)


def spatial_kernel(at_ref, tokens_same_ref, tokens_cross_ref, same_ref, cross_ref, same_y_ref, cross_y_ref, out_ref, picked_ref, wide_ref, normed_ref, all_ref):
    tokens_kernel(at_ref, tokens_same_ref, tokens_cross_ref, normed_ref, picked_ref, all_ref)
    pieces = []
    for dy, same, cross in ((0, same_ref, cross_ref), (1, same_y_ref, cross_y_ref)):
        for d in range(4):
            pieces += [(d, dy, 0, same[d, 0]), (d, dy, 1, cross[d])]
    w = unpack(at_ref, pieces, wide_ref)
    packed = jnp.dot(normed_ref[...], w, preferred_element_type=jnp.float32).astype(jnp.bfloat16)
    n = packed.shape[0]
    row = lax.broadcasted_iota(jnp.int32, (n, n), 0) // 32
    col = lax.broadcasted_iota(jnp.int32, (n, n), 1) // 32
    out_ref[...] = fold(masked_attention(packed, row == col))


def project(y, heads, own_ref, other_ref):
    own, other = (
        lax.dot_general(heads, ref[...], (((1,), (1,)), ((), ())), preferred_element_type=jnp.float32) for ref in (own_ref, other_ref)
    )
    return jnp.concatenate([jnp.where(y == 0, own, other), jnp.where(y == 0, other, own)], axis=1)


def mixed_kernel(at_ref, same_ref, cross_ref, picked_ref, own_ref, other_ref, keep_ref, send_ref, all_ref):
    y = at_ref[0]
    assemble(at_ref, same_ref, cross_ref, all_ref)
    update = project(y, heads_of(all_ref), own_ref, other_ref)
    mixed = picked_ref[...].astype(jnp.float32) + update
    for j in range(8):
        low, high = mixed[32 * j : 32 * j + 16], mixed[32 * j + 16 : 32 * j + 32]
        keep_ref[16 * j : 16 * j + 16, :] = jnp.where(y == 0, low, high).astype(jnp.bfloat16)
        send_ref[16 * j : 16 * j + 16, :] = jnp.where(y == 0, high, low).astype(jnp.bfloat16)


def rows_kernel(at_ref, mine_ref, theirs_ref, out_ref, wide_ref):
    y = at_ref[0]
    for half, ref in ((y, mine_ref), (1 - y, theirs_ref)):
        for j in range(8):
            slab = ref[j].astype(jnp.float32)
            first = pl.multiple_of(176 * j + 88 * half, 8)
            for g in range(11):
                wide_ref[pl.ds(first + 8 * g, 8), :] = slab[:, 264 * g : 264 * (g + 1)]
    out_ref[...] = wide_ref[...].astype(jnp.bfloat16)


def temporal_kernel(at_ref, same_ref, cross_ref, mine_ref, theirs_ref, out_ref, all_ref, w_ref, wide_ref):
    rows_kernel(at_ref, mine_ref, theirs_ref, w_ref, wide_ref)
    assemble(at_ref, same_ref, cross_ref, all_ref)
    own = jnp.concatenate([all_ref[j][:, :176] for j in range(8)], axis=1)
    other = jnp.concatenate([all_ref[j][:, 176:] for j in range(8)], axis=1)
    mixed = jnp.concatenate([own, other], axis=0)
    packed = jnp.dot(normalize(mixed), w_ref[...], preferred_element_type=jnp.float32).astype(jnp.bfloat16)
    n = packed.shape[0]
    row = lax.broadcasted_iota(jnp.int32, (n, n), 0) % 16
    col = lax.broadcasted_iota(jnp.int32, (n, n), 1) % 16
    out_ref[...] = fold(masked_attention(packed, row == col))


def result_kernel(at_ref, same_ref, cross_ref, mixed_ref, own_ref, other_ref, out_ref, all_ref):
    y = at_ref[0]
    assemble(at_ref, same_ref, cross_ref, all_ref)
    update = project(y, heads_of(all_ref), own_ref, other_ref)
    for half in range(2):
        for j in range(8):
            frame = 4 * (j // 2) + 2 * (y if half == 0 else 1 - y) + j % 2
            residual = mixed_ref[16 * j : 16 * j + 16, 176 * half : 176 * (half + 1)].astype(jnp.float32)
            at = 128 * half + 16 * j
            rows = (residual + update[at : at + 16]).astype(jnp.bfloat16)
            out_ref[frame] = jnp.concatenate([rows[:8], rows[8:]], axis=1)


def finish_kernel(blocks_ref, out_ref):
    for i in range(16):
        z, y, k = i // 4, (i // 2) % 2, i % 2
        block = blocks_ref[i]
        for other in range(2):
            at = 88 * (4 * z + 2 * other + k)
            for half in range(2):
                first = 16 * y + 8 * half
                out_ref[first : first + 8, at : at + 88] = block[:, 176 * half + 88 * other : 176 * half + 88 * (other + 1)]


VM = pl.BlockSpec(memory_space=pltpu.VMEM)
SM = pl.BlockSpec(memory_space=pltpu.SMEM)


def kernel_call(body, shapes, n_in, scratch=(), scalar=False):
    return pl.pallas_call(
        body,
        out_shape=shapes,
        in_specs=([SM] if scalar else []) + [VM] * n_in,
        out_specs=jax.tree.map(lambda _: VM, shapes),
        scratch_shapes=scratch,
        compiler_params=pltpu.CompilerParams(vmem_limit_bytes=40 * 1024 * 1024),
    )


def to(mask):
    return [(i, i ^ mask) for i in range(16)]


def head_body(video, spatial_qkv, spatial_out, temporal_qkv, temporal_out):
    _, patches, D = video.shape
    bf = jnp.bfloat16
    place = lax.axis_index("seq")
    at = jnp.stack([(place // 2) % 2, place // 4, place % 2])
    scatter = lambda a: lax.all_to_all(a, "seq", 0, 0, tiled=True, axis_index_groups=COLUMNS)
    across = lambda a: lax.ppermute(a, "seq", ACROSS_Y)

    def gather(a):
        far, mid, near = (lax.ppermute(a, "seq", to(m)) for m in (12, 8, 4))
        same = jnp.stack([a, near, mid, far])
        return same, lax.ppermute(same, "seq", to(1))

    def call(body, shapes, *args, scratch=()):
        return kernel_call(body, shapes, len(args), list(scratch), True)(at, *args)

    S = lambda *shape: jax.ShapeDtypeStruct(shape, bf)
    wide = pltpu.VMEM((D, 264), jnp.float32)
    heads = pltpu.VMEM((8, 64, 352), bf)

    so, to_ = spatial_out.T, temporal_out.T
    part = S(2, 8, 11 * 264)
    parts = call(pack_near_kernel, (part,) * 4, spatial_qkv, scratch=[pltpu.VMEM((4, 2, 8, 11 * 264), bf)])
    near, mid, far = (lax.ppermute(p, "seq", to(m)) for p, m in zip(parts[1:], (4, 8, 12)))
    so_o, to_o = across(so), across(to_)
    near, mid, far, so_o, to_o, frame, packed_two = lax.optimization_barrier(
        (near, mid, far, so_o, to_o, video.reshape(patches, D), pack_call(temporal_qkv))
    )
    all_w = jnp.stack([parts[0], near, mid, far])
    all_y = across(all_w)
    cross_w = lax.ppermute(all_w[:, 1], "seq", to(1))
    two_w = scatter(packed_two)
    t_far, t_mid, t_near = (lax.ppermute(frame, "seq", to(m)) for m in (12, 8, 4))
    same = jnp.stack([frame, t_near, t_mid, t_far])
    same, all_y = lax.optimization_barrier((same, all_y))
    tokens = same, lax.ppermute(same, "seq", to(1))
    cross_y = lax.ppermute(all_y[:, 1], "seq", to(1))
    spatial, picked = call(
        spatial_kernel, (S(64, 352), S(256, 176)), *tokens, all_w, cross_w, all_y, cross_y,
        scratch=[wide, pltpu.VMEM((256, D), bf), pltpu.VMEM((8, patches, D), bf)],
    )
    same, cross = gather(spatial)
    same, two_w = lax.optimization_barrier((same, two_w))
    two_o = across(two_w)
    keep, send = call(mixed_kernel, (S(128, 176), S(128, 176)), same, cross, picked, so, so_o, scratch=[heads])
    mixed = jnp.concatenate([keep, across(send)], axis=1)
    temporal = call(
        temporal_kernel, S(64, 352), *gather(mixed), two_w, two_o, scratch=[pltpu.VMEM((8, 128, 352), bf), pltpu.VMEM((D, 264), bf), wide]
    )
    result = call(result_kernel, S(16, 8, 352), *gather(temporal), mixed, to_, to_o, scratch=[heads])
    result = lax.all_to_all(result, "seq", 0, 0, tiled=True)
    return kernel_call(finish_kernel, S(patches, D), 1)(result).reshape(1, patches, D)


def solution(mesh):
    in_specs = (
        P(("groups", "seq"), None, None),
        P("seq", None),
        P(None, "seq"),
        P("seq", None),
        P(None, "seq"),
    )
    out_specs = P(("groups", "seq"), None, None)
    body = head_body if mesh.shape["seq"] == 16 else gathered_weights_body
    return jax.shard_map(body, mesh=mesh, in_specs=in_specs, out_specs=out_specs, check_vma=False)
```
